32 devices in a mesh: dp: 2 (over y), ctx: 16 (over z, x, core).
Axes of the slice: x: 2, y: 2, z: 4, core: 2. Of those that a mesh axis runs over, the one named last changes fastest.
Arguments:
- tokens: bfloat16 [2, 2048, 2048], P('dp', 'ctx'), may hold values from -6 to 6
- cotangent: bfloat16 [2, 2048, 2048], P('dp', 'ctx'), may hold values from -6 to 6
- norm_gains: float32 [2, 2048], replicated, may hold values from 0.1 to 1.9
- head_gains: float32 [2, 64], replicated, may hold values from 1 to 2
- input_weight: float32 [2048, 2304], P(('dp', 'ctx')), may hold values from -0.125 to 0.125
- output_weight: float32 [1536, 2048], P(('dp', 'ctx')), may hold values from -1.25 to 1.25
- expand_weight: float32 [2048, 10240], P(('dp', 'ctx')), may hold values from -0.125 to 0.125
- reduce_weight: float32 [5120, 2048], P(('dp', 'ctx')), may hold values from -0.078125 to 0.078125
- norm_moment: float32 [2, 2048], replicated, may hold values from -6 to 6
- head_moment: float32 [2, 64], replicated, may hold values from -6 to 6
- input_moment: float32 [2048, 2304], P(('dp', 'ctx')), may hold values from -6 to 6
- output_moment: float32 [1536, 2048], P(('dp', 'ctx')), may hold values from -6 to 6
- expand_moment: float32 [2048, 10240], P(('dp', 'ctx')), may hold values from -6 to 6
- reduce_moment: float32 [5120, 2048], P(('dp', 'ctx')), may hold values from -6 to 6
- learn_rate: float32 [], replicated, may hold values from 0.05 to 0.2
Outputs:
- layer_out: bfloat16 [2, 2048, 2048], P('dp', 'ctx')
- token_grad: bfloat16 [2, 2048, 2048], P('dp', 'ctx')
- grad_norm: float32 [], replicated
- moment_norms: float32 [2, 2048], replicated
- moment_heads: float32 [2, 64], replicated
- moment_input: float32 [2048, 2304], P(('dp', 'ctx'))
- moment_output: float32 [1536, 2048], P(('dp', 'ctx'))
- moment_expand: float32 [2048, 10240], P(('dp', 'ctx'))
- moment_reduce: float32 [5120, 2048], P(('dp', 'ctx'))
- next_norms: float32 [2, 2048], replicated
- next_heads: float32 [2, 64], replicated
- next_input: float32 [2048, 2304], P(('dp', 'ctx'))
- next_output: float32 [1536, 2048], P(('dp', 'ctx'))
- next_expand: float32 [2048, 10240], P(('dp', 'ctx'))
- next_reduce: float32 [5120, 2048], P(('dp', 'ctx'))
The draws below stay inside these ranges and needn't reach their ends.
All inputs are finite; a program needn't handle non-finite values.
Results may differ from the reference program's by a relative error of at most 0.03.
Values may be sent and summed in bfloat16 or wider, within the bound.
A program may use at most 320 MiB of HBM per device.

```python
import math
import jax
import jax.numpy as jnp
from jax import lax

D = 2048
HEADS = 24
KV_HEADS = 6
HD = 64
FF = 5120
GROUP = 4
QKV = 2304
LEN = 2048
SEQ_ALL = 2
NPARAM = 39325824


def spiked(drawn, stream_key, source, target, blocks, factor):
    owner, partner = [(jnp.arange(drawn.shape[dim]) // (drawn.shape[dim] // blocks)).reshape([-1 if axis == dim else 1 for axis in range(drawn.ndim)]) for dim in (source, target)]
    chosen = jax.random.permutation(stream_key, blocks)[partner]
    strong = (owner == chosen) | (owner == (partner + blocks // 2) % blocks)
    return jnp.where(strong, factor * drawn, drawn)


def steps_of(stream_key, extent, shards, low, high):
    gain, own = 1.0, jax.random.fold_in(stream_key, 6)
    for dim, parts in shards:
        draws = jnp.exp(jax.random.uniform(jax.random.fold_in(own, dim), (parts,), jnp.float32, low / len(shards), high / len(shards)))
        gain = gain * jnp.repeat(draws, extent[dim] // parts).reshape([-1 if axis == dim else 1 for axis in range(len(extent))])
    return gain


def gaussian(rng, extent, deviation, most, pieces=(), dtype=jnp.bfloat16):
    drawn = deviation * jax.random.normal(rng, extent, jnp.float32)
    if pieces:
        drawn = drawn * steps_of(rng, extent, pieces, -0.22, 0.18)
    return jnp.clip(drawn, -most, most).astype(dtype)


def gaussian_with(rng, dims, deviation, most, pieces, heavy, kind=jnp.bfloat16):
    array = deviation * jax.random.normal(rng, dims, jnp.float32)
    if pieces:
        array = array * steps_of(rng, dims, pieces, -0.22, 0.18)
    return jnp.clip(spiked(array, jax.random.fold_in(rng, 3), *heavy), -most, most).astype(kind)


def setup_inputs(seed: int = 0) -> dict:
    key_of = jax.random.split(jax.random.key(seed), 16)
    tokens = gaussian_with(key_of[0], (SEQ_ALL, LEN, D), 1.0, 6.0, ((0, 2), (1, 16)), (1, 2, 16, 2.0))
    cotangent = gaussian(key_of[1], (SEQ_ALL, LEN, D), 1.0, 6.0, ((0, 2), (1, 16)))
    norm_gains = jnp.clip(1.0 + 0.18 * jax.random.normal(key_of[2], (2, D), jnp.float32), 0.1, 1.9)
    head_gains = jnp.clip(jax.random.uniform(key_of[3], (2, HD), jnp.float32, 1.0, 2.0), 1.0, 2.0)
    input_weight = gaussian(key_of[4], (D, QKV), D ** -0.5, 0.125, ((0, 32),), jnp.float32)
    output_weight = gaussian(key_of[5], (HEADS * HD, D), (HEADS * HD // 64) ** -0.5, 1.25, ((0, 32),), jnp.float32)
    expand_weight = gaussian(key_of[6], (D, 2 * FF), D ** -0.5, 0.125, ((0, 32),), jnp.float32)
    reduce_weight = gaussian(key_of[7], (FF, D), FF ** -0.5, 0.078125, ((0, 32),), jnp.float32)
    norm_moment = gaussian(key_of[8], (2, D), 1.0, 6.0, (), jnp.float32)
    head_moment = gaussian(key_of[9], (2, HD), 1.0, 6.0, (), jnp.float32)
    input_moment = gaussian(key_of[10], (D, QKV), 1.0, 6.0, ((0, 32),), jnp.float32)
    output_moment = gaussian(key_of[11], (HEADS * HD, D), 1.0, 6.0, ((0, 32),), jnp.float32)
    expand_moment = gaussian(key_of[12], (D, 2 * FF), 1.0, 6.0, ((0, 32),), jnp.float32)
    reduce_moment = gaussian(key_of[13], (FF, D), 1.0, 6.0, ((0, 32),), jnp.float32)
    learn_rate = jnp.clip(jax.random.uniform(key_of[14], (), jnp.float32, 0.05, 0.2), 0.05, 0.2)
    return dict(tokens=tokens, cotangent=cotangent, norm_gains=norm_gains, head_gains=head_gains, input_weight=input_weight, output_weight=output_weight, expand_weight=expand_weight, reduce_weight=reduce_weight, norm_moment=norm_moment, head_moment=head_moment, input_moment=input_moment, output_moment=output_moment, expand_moment=expand_moment, reduce_moment=reduce_moment, learn_rate=learn_rate)


EPSILON = 1e-06
THETA = 10000.0
NEGATIVE = -1e+30
MOMENTUM = 0.5
HIGHEST = lax.Precision.HIGHEST

@jax.custom_vjp
def low(v):
    return lax.optimization_barrier(v.astype(jnp.bfloat16)).astype(jnp.float32)

@jax.custom_vjp
def low_back(v):
    return v

def low_keep(v):
    return (low(v), None)

def low_pass(kept, grad):
    return (grad,)

def back_keep(v):
    return (v, None)

def back_low(kept, grad):
    return (low(grad),)
low.defvjp(low_keep, low_pass)
low_back.defvjp(back_keep, back_low)

def rms_normed(values, gains):
    mean_square = lax.optimization_barrier(jnp.mean(values * values, axis=-1, keepdims=True))
    return values * lax.rsqrt(mean_square + EPSILON) * gains

def rotary(values, positions):
    half_width = values.shape[-1] // 2
    frequency = THETA ** (-2.0 * jnp.arange(half_width).astype(jnp.float32) / values.shape[-1])
    angles = positions.astype(jnp.float32)[:, None] * frequency[None, :]
    cosine = jnp.cos(angles)[:, None, :]
    sine_rows = jnp.sin(angles)[:, None, :]
    front_half = values[..., :half_width]
    back_half = values[..., half_width:]
    return jnp.concatenate([front_half * cosine - back_half * sine_rows, back_half * cosine + front_half * sine_rows], axis=-1)

def prepare(projected, head_gains, positions):
    row_count = projected.shape[0]
    queries = projected[:, :HEADS * HD].reshape(row_count, HEADS, HD)
    key_rows = projected[:, HEADS * HD:(HEADS + KV_HEADS) * HD].reshape(row_count, KV_HEADS, HD)
    value_rows = projected[:, (HEADS + KV_HEADS) * HD:].reshape(row_count, KV_HEADS, HD)
    queries = rotary(rms_normed(queries, head_gains[0]), positions)
    key_rows = rotary(rms_normed(key_rows, head_gains[1]), positions)
    return (queries, key_rows, value_rows)

def attend_block(query_block, block_start, key_rows, value_rows):
    block_width = query_block.shape[0]
    grouped = query_block.reshape(block_width, KV_HEADS, GROUP, HD)
    scores = low_back(jnp.einsum('qkgd,nkd->kgqn', grouped, key_rows, precision=HIGHEST) / math.sqrt(HD))
    query_pos = block_start + jnp.arange(block_width).astype(jnp.int32)
    key_pos = jnp.arange(key_rows.shape[0]).astype(jnp.int32)
    allowed = key_pos[None, :] <= query_pos[:, None]
    scores = jnp.where(allowed, scores, NEGATIVE)
    prob_rows = jax.nn.softmax(scores, axis=-1)
    attended = jnp.einsum('kgqn,nkd->qkgd', low(prob_rows), value_rows, precision=HIGHEST)
    return attended.reshape(block_width, HEADS * HD)

def attention(queries, key_rows, value_rows):
    block_width = min(512, LEN)
    block_count = LEN // block_width
    query_blocks = queries.reshape(block_count, block_width, HEADS, HD)
    block_starts = (jnp.arange(block_count) * block_width).astype(jnp.int32)

    def one_block(pair_in):
        return attend_block(pair_in[0], pair_in[1], key_rows, value_rows)
    attended = lax.map(jax.checkpoint(one_block), (query_blocks, block_starts))
    return attended.reshape(LEN, HEADS * HD)

def layer(params, sequence):
    norm_gains, head_gains, input_weight, output_weight, expand_weight, reduce_weight = params
    positions = jnp.arange(LEN).astype(jnp.int32)
    normed_one = low(rms_normed(sequence, norm_gains[0]))
    projected = low_back(jnp.dot(normed_one, input_weight, precision=HIGHEST, preferred_element_type=jnp.float32))
    queries, key_rows, value_rows = prepare(projected, head_gains, positions)
    attended = attention(low(queries), low(key_rows), low(value_rows))
    attended = low(low_back(attended))
    branch = low_back(jnp.dot(attended, output_weight, precision=HIGHEST, preferred_element_type=jnp.float32))
    residual = sequence + branch
    normed_two = low(rms_normed(residual, norm_gains[1]))
    expanded = low_back(jnp.dot(normed_two, expand_weight, precision=HIGHEST, preferred_element_type=jnp.float32))
    hidden = low(jax.nn.silu(expanded[:, :FF]) * expanded[:, FF:])
    return residual + jnp.dot(hidden, reduce_weight, precision=HIGHEST, preferred_element_type=jnp.float32)

def reference(tokens, cotangent, norm_gains, head_gains, input_weight, output_weight, expand_weight, reduce_weight, norm_moment, head_moment, input_moment, output_moment, expand_moment, reduce_moment, learn_rate):
    params = (norm_gains, head_gains, input_weight, output_weight, expand_weight, reduce_weight)
    moments = (norm_moment, head_moment, input_moment, output_moment, expand_moment, reduce_moment)
    zero_grads = jax.tree.map(jnp.zeros_like, params)

    def one_sequence(totals, inputs):
        sequence, upstream = inputs
        result, pullback = jax.vjp(layer, params, sequence.astype(jnp.float32))
        layer_grads, sequence_grad = pullback(upstream.astype(jnp.float32))
        totals = jax.tree.map(jnp.add, totals, layer_grads)
        return (totals, (result.astype(jnp.bfloat16), sequence_grad.astype(jnp.bfloat16)))
    totals, outputs = lax.scan(one_sequence, zero_grads, (tokens, cotangent))
    layer_out, token_grad = outputs
    squares = sum((jnp.sum(entry * entry) for entry in totals))
    grad_norm = jnp.sqrt(squares)
    clip_limit = math.sqrt(NPARAM)
    factor = clip_limit / jnp.maximum(grad_norm, clip_limit)
    new_moments = tuple((MOMENTUM * moment + factor * gradient for moment, gradient in zip(moments, totals)))
    updated = tuple((weight - learn_rate * moment for weight, moment in zip(params, new_moments)))
    return (layer_out, token_grad, grad_norm, new_moments[0], new_moments[1], new_moments[2], new_moments[3], new_moments[4], new_moments[5], updated[0], updated[1], updated[2], updated[3], updated[4], updated[5])
```

```python
import functools
import math

import jax
import jax.numpy as jnp
from jax import lax
from jax.experimental import pallas as pl
from jax.experimental.pallas import tpu as pltpu
from jax.sharding import Mesh
from jax.sharding import PartitionSpec as P

HEADS = 24
KV_HEADS = 6
HD = 64
FF = 5120
GROUP = 4
NPARAM = 39325824


EPSILON = 1e-06
THETA = 10000.0
MOMENTUM = 0.5

BF = jnp.bfloat16
F32 = jnp.float32
WIDE = 2 * HD
CHAIN = 4
CORES = 2
AXES = ("dp", "a", "b", "c")
ANY = pl.BlockSpec(memory_space=pl.ANY)
VMEM = pl.BlockSpec(memory_space=pltpu.VMEM)
NT = (((1,), (1,)), ((), ()))
TN = (((0,), (0,)), ((), ()))
NN = (((1,), (0,)), ((), ()))


def mm(left, right, dims):
    return lax.dot_general(left, right, dims, preferred_element_type=F32)


class Here:
    def __init__(self):
        self.y, self.a, self.b, self.c = (lax.axis_index(name) for name in AXES)
        self.dp, self.chain, self.mid, self.cores = (lax.axis_size(name) for name in AXES)
        self.rank = (self.a * self.mid + self.b) * self.cores + self.c
        self.shard = self.y * (self.chain * self.mid * self.cores) + self.rank

    def to(self, y=0, a=0, b=0, c=0):
        out = {}
        for name, mine, offset in zip(AXES, (self.y, self.a, self.b, self.c), (y, a, b, c)):
            out[name] = mine ^ offset if offset else mine
        return out

    def plane(self):
        return [
            (y, b) for y in range(self.dp) for b in range(self.mid) if y or b
        ]


def greet(here, offsets):
    barrier = pltpu.get_barrier_semaphore()
    for offset in offsets:
        pl.semaphore_signal(
            barrier, inc=1, device_id=here.to(**offset), device_id_type=pl.DeviceIdType.MESH
        )
    pl.semaphore_wait(barrier, len(offsets))


class Wire:
    def __init__(self, send, recv):
        self.send, self.recv, self.made = send, recv, []

    def push(self, source, target, device):
        k = len(self.made)
        copy = pltpu.make_async_remote_copy(
            src_ref=source,
            dst_ref=target,
            send_sem=self.send.at[k],
            recv_sem=self.recv.at[k],
            device_id=device,
            device_id_type=pl.DeviceIdType.MESH,
        )
        copy.start()
        self.made.append(copy)
        return copy

    def drain(self):
        for copy in self.made:
            copy.wait_send()


def wires(count):
    return [pltpu.SemaphoreType.DMA((count,)), pltpu.SemaphoreType.DMA((count,))]


def chain_offsets(here):
    return [dict(a=o) for o in range(1, here.chain)]


def plane_offsets(here):
    return [dict(y=y, b=b) for y, b in here.plane()]


def block_offsets(here):
    return [
        dict(y=y, b=b, c=c)
        for y in range(here.dp)
        for b in range(here.mid)
        for c in range(here.cores)
        if y or b or c
    ]


class Gather:
    def __init__(self, here, wire, shard, full):
        self.here, self.wire, self.shard, self.full = here, wire, shard, full
        self.core = []

    @staticmethod
    def copies(dp, chain, mid):
        return (chain - 1) + (dp * mid - 1) * chain + dp * chain * mid

    def spread(self, source, slot):
        h = self.here
        made = {
            (y, b): self.wire.push(source, slot, h.to(y=y, b=b)) for y, b in h.plane()
        }
        self.core.append(self.wire.push(source, slot, h.to(c=1)))
        return made

    def start(self):
        h = self.here
        slot = self.full.at[h.y, h.a, h.b, h.c]
        self.chain = {
            o: self.wire.push(self.shard, slot, h.to(a=o)) for o in range(1, h.chain)
        }
        self.sheet = {0: self.spread(self.shard, slot)}

    def relay_chain(self):
        h = self.here
        for o in range(1, h.chain):
            self.chain[o].wait_recv()
            slot = self.full.at[h.y, h.a ^ o, h.b, h.c]
            self.sheet[o] = self.spread(slot, slot)

    def relay_plane(self):
        h = self.here
        for o in range(h.chain):
            for y, b in h.plane():
                self.sheet[o][y, b].wait_recv()
                slot = self.full.at[h.y ^ y, h.a ^ o, h.b ^ b, h.c]
                self.core.append(self.wire.push(slot, slot, h.to(c=1)))

    def finish(self):
        for copy in self.core:
            copy.wait_recv()


def call(body, outs, ins, scratch, ident, out_specs, in_specs, sent=0):
    return pl.pallas_call(
        body,
        out_shape=outs,
        in_specs=in_specs,
        out_specs=out_specs,
        scratch_shapes=scratch,
        compiler_params=pltpu.CompilerParams(collective_id=ident, has_side_effects=True),
        cost_estimate=pl.CostEstimate(flops=0, bytes_accessed=sent, transcendentals=0),
    )(*ins)


def chunk_columns(chunk, part, width):
    start = part * FF + chunk * width
    return pl.ds(pl.multiple_of(start, 128), width)


def first_kernel(win_ref, ex_ref, win_out, e1_out, send, recv, local):
    h = Here()
    width = FF // (h.chain * h.cores)
    greet(h, [dict(a=a, c=c) for a in range(h.chain) for c in range(h.cores) if a or c] + plane_offsets(h))
    wire = Wire(send, recv)
    own = pltpu.make_async_copy(win_ref, win_out.at[h.y, h.a, h.b, h.c], local.at[0])
    own.start()
    gather = Gather(h, wire, win_ref, win_out)
    gather.start()
    kept = []
    for part in range(2):
        mine = ex_ref.at[:, chunk_columns(h.c * h.chain + h.a, part, width)]
        spot = e1_out.at[h.a, h.c, :, pl.ds(part * width, width)]
        copy = pltpu.make_async_copy(mine, spot, local.at[1 + part])
        copy.start()
        kept.append(copy)
    swaps = []
    for a in range(h.chain):
        for c in range(h.cores):
            if not (a or c):
                continue
            for part in range(2):
                chunk = (h.c ^ c) * h.chain + (h.a ^ a)
                source = ex_ref.at[:, chunk_columns(chunk, part, width)]
                spot = e1_out.at[h.a, h.c, :, pl.ds(part * width, width)]
                swaps.append(wire.push(source, spot, h.to(a=a, c=c)))
    gather.relay_chain()
    gather.relay_plane()
    gather.finish()
    for copy in swaps:
        copy.wait_recv()
    wire.drain()
    own.wait()
    for copy in kept:
        copy.wait()


def gather_first(win, ex, sizes):
    dp, chain, mid, cores = sizes
    rows = win.shape[0]
    width = 2 * FF // (chain * cores)
    count = Gather.copies(dp, chain, mid) + 2 * (chain * cores - 1)
    return call(
        first_kernel,
        (
            jax.ShapeDtypeStruct((dp, chain, mid, cores) + win.shape, BF),
            jax.ShapeDtypeStruct((chain, cores, rows, width), BF),
        ),
        (win, ex),
        wires(count) + [pltpu.SemaphoreType.DMA((3,))],
        1,
        (ANY, ANY),
        [ANY, ANY],
    )


def masked(values, pair, rank, span):
    key_pos = pair * (2 * span) + lax.broadcasted_iota(jnp.int32, values.shape, 0)
    query_pos = rank * span + lax.rem(lax.broadcasted_iota(jnp.int32, values.shape, 1), span)
    return jnp.where(key_pos <= query_pos, values, 0.0)


def second_kernel(
    q_ref, kv_ref, wout_ref, cot_ref, o_ref, lse_ref, kv_out, wout_out, cot_out,
    kv_all, send, recv, local,
):
    h = Here()
    span = kv_ref.shape[1]
    greet(
        h,
        chain_offsets(h) + plane_offsets(h) + [dict(c=1)],
    )
    wire = Wire(send, recv)
    own_out = pltpu.make_async_copy(wout_ref, wout_out.at[h.y, h.a, h.b, h.c], local.at[0])
    own_out.start()
    own_cot = pltpu.make_async_copy(cot_ref, cot_out.at[h.a, h.c], local.at[1])
    own_cot.start()

    def block(a, b, c):
        return kv_all.at[((h.a ^ a) * h.mid + (h.b ^ b)) * h.cores + (h.c ^ c)]

    mine = block(0, 0, 0)
    mine[...] = kv_ref[...]
    core = []
    chain = {o: wire.push(kv_ref, mine, h.to(a=o)) for o in range(1, h.chain)}
    side = {(0, b): wire.push(kv_ref, mine, h.to(b=b)) for b in range(1, h.mid)}
    core.append(wire.push(kv_ref, mine, h.to(c=1)))
    gather = Gather(h, wire, wout_ref, wout_out)
    for o in range(1, h.chain):
        chain[o].wait_recv()
        spot = block(o, 0, 0)
        for b in range(1, h.mid):
            side[o, b] = wire.push(spot, spot, h.to(b=b))
        core.append(wire.push(spot, spot, h.to(c=1)))
    gather.start()
    cots = {o: wire.push(cot_ref, cot_out.at[h.a, h.c], h.to(a=o)) for o in range(1, h.chain)}
    cot_core = [wire.push(cot_ref, cot_out.at[h.a, h.c], h.to(c=1))]
    for o in range(h.chain):
        for b in range(1, h.mid):
            side[o, b].wait_recv()
            spot = block(o, b, 0)
            core.append(wire.push(spot, spot, h.to(c=1)))
    gather.relay_chain()
    for copy in core:
        copy.wait_recv()
    store = pltpu.make_async_copy(kv_all, kv_out, local.at[2])
    store.start()

    last = h.rank // 2

    def head(g, unused):
        query = q_ref[g]

        def visit(pair, hide):
            keys = kv_all[pl.ds(2 * pair, 2), g].reshape(2 * span, WIDE)
            weights = jnp.exp(mm(keys, query, NT))
            if hide:
                weights = masked(weights, pair, h.rank, span)
            total = jnp.sum(weights, axis=0, keepdims=True)
            return total, mm(keys, weights.astype(BF), TN)[HD:]

        total, value = visit(last, True)
        lse_ref[g] = total
        o_ref[g] = value

        def step(pair, unused_inner):
            total, value = visit(pair, False)
            lse_ref[g] += total
            o_ref[g] += value
            return unused_inner

        lax.fori_loop(0, last, step, 0)
        o_ref[g] = o_ref[g] / lse_ref[g]
        lse_ref[g] = jnp.log(lse_ref[g])
        return unused

    lax.fori_loop(0, KV_HEADS, head, 0)
    gather.relay_plane()
    for o in range(1, h.chain):
        cots[o].wait_recv()
        spot = cot_out.at[h.a ^ o, h.c]
        cot_core.append(wire.push(spot, spot, h.to(c=1)))
    gather.finish()
    for copy in cot_core:
        copy.wait_recv()
    wire.drain()
    own_out.wait()
    own_cot.wait()
    store.wait()


def attend_forward(query, kv, wout, cot, sizes):
    dp, chain, mid, cores = sizes
    blocks = chain * mid * cores
    rows = query.shape[1]
    count = (
        (chain - 1) + (mid - 1) * chain + chain * mid
        + Gather.copies(dp, chain, mid) + 2 * (chain - 1) + 1
    )
    return call(
        second_kernel,
        (
            jax.ShapeDtypeStruct((KV_HEADS, HD, rows), F32),
            jax.ShapeDtypeStruct((KV_HEADS, 1, rows), F32),
            jax.ShapeDtypeStruct((blocks,) + kv.shape, BF),
            jax.ShapeDtypeStruct((dp, chain, mid, cores) + wout.shape, BF),
            jax.ShapeDtypeStruct((chain, cores) + cot.shape, BF),
        ),
        (query, kv, wout, cot),
        [pltpu.VMEM((blocks,) + kv.shape, BF)] + wires(count) + [pltpu.SemaphoreType.DMA((3,))],
        2,
        (VMEM, VMEM, ANY, ANY, ANY),
        [VMEM, VMEM, ANY, ANY],
    )


def third_kernel(n_ref, e1_ref, rd_ref, n_out, ex_out, rd_out, send, recv, rsend, rrecv, local):
    h = Here()
    greet(h, chain_offsets(h) + block_offsets(h))
    wire = Wire(send, recv)
    own = pltpu.make_async_copy(n_ref, n_out.at[h.a, h.c], local.at[0])
    own.start()
    rows = {o: wire.push(n_ref, n_out.at[h.a, h.c], h.to(a=o)) for o in range(1, h.chain)}
    core = [wire.push(n_ref, n_out.at[h.a, h.c], h.to(c=1))]
    kept, sheets = [], []
    for a in range(h.chain):
        for y, b in h.plane():
            sheets.append(wire.push(e1_ref.at[a], ex_out.at[h.y, a, h.b], h.to(y=y, b=b)))
        copy = pltpu.make_async_copy(e1_ref.at[a], ex_out.at[h.y, a, h.b], local.at[1 + a])
        copy.start()
        kept.append(copy)
    slot = h.b * h.cores + h.c

    def reduce_copy(number, y, b):
        device = h.to(y=y, b=b)
        device["c"] = h.y
        return pltpu.make_async_remote_copy(
            src_ref=rd_ref,
            dst_ref=rd_out.at[h.b, h.c],
            send_sem=rsend.at[number],
            recv_sem=rrecv.at[slot],
            device_id=device,
            device_id_type=pl.DeviceIdType.MESH,
        )

    far = [reduce_copy(1 + i, y, b) for i, (y, b) in enumerate(h.plane())]
    for copy in far:
        copy.start()

    @pl.when(h.c == h.y)
    def _():
        pltpu.make_async_copy(rd_ref, rd_out.at[h.b, h.c], rrecv.at[slot]).start()

    @pl.when(h.c != h.y)
    def _():
        reduce_copy(0, 0, 0).start()

    for o in range(1, h.chain):
        rows[o].wait_recv()
        spot = n_out.at[h.a ^ o, h.c]
        core.append(wire.push(spot, spot, h.to(c=1)))
    for copy in core:
        copy.wait_recv()
    for copy in sheets:
        copy.wait_recv()
    for b in range(h.mid):
        for c in range(h.cores):
            spot = rd_out.at[b, c]
            pltpu.make_async_copy(spot, spot, rrecv.at[b * h.cores + c]).wait()
    wire.drain()
    for copy in far:
        copy.wait_send()

    @pl.when(h.c != h.y)
    def _():
        reduce_copy(0, 0, 0).wait_send()

    own.wait()
    for copy in kept:
        copy.wait()


def gather_feed(normed, e1, rd, sizes):
    dp, chain, mid, cores = sizes
    count = 2 * (chain - 1) + 1 + chain * (dp * mid - 1)
    return call(
        third_kernel,
        (
            jax.ShapeDtypeStruct((chain, cores) + normed.shape, BF),
            jax.ShapeDtypeStruct((dp, chain, mid) + e1.shape[1:], BF),
            jax.ShapeDtypeStruct((mid, cores) + rd.shape, BF),
        ),
        (normed, e1, rd),
        wires(count)
        + [pltpu.SemaphoreType.DMA((dp * mid,)), pltpu.SemaphoreType.DMA((mid * cores,))]
        + [pltpu.SemaphoreType.DMA((1 + chain,))],
        3,
        (ANY, ANY, ANY),
        [ANY, ANY, ANY],
    )


class Fold:
    def __init__(self, here, wire, part, near, half, far):
        self.here, self.wire, self.part = here, wire, part
        self.near, self.half, self.far = near, half, far

    @staticmethod
    def copies(chain):
        return chain + chain - 1

    @staticmethod
    def scratch(part):
        chain, cores, rows, width = part.shape
        return [pltpu.VMEM((chain, rows, width), BF) for _ in range(3)]

    def start(self):
        h = self.here
        self.swap = {
            o: self.wire.push(self.part.at[h.a ^ o, h.c ^ 1], self.near.at[o], h.to(c=1))
            for o in list(range(1, h.chain)) + [0]
        }

    def pass_on(self):
        h = self.here
        self.sent = {}
        rows = self.part.shape[2]
        for o in range(1, h.chain):
            self.swap[o].wait_recv()

            def add(i, unused):
                at = pl.ds(pl.multiple_of(i * 16, 16), 16)
                both = self.part[h.a ^ o, h.c, at].astype(F32) + self.near[o, at].astype(F32)
                self.half[o, at] = both.astype(BF)
                return unused

            lax.fori_loop(0, rows // 16, add, 0)
            self.sent[o] = self.wire.push(self.half.at[o], self.far.at[o], h.to(a=o))
        self.swap[0].wait_recv()

    def finish(self, out):
        h = self.here
        rows = self.part.shape[2]
        for o in range(1, h.chain):
            self.sent[o].wait_recv()

        def add(i, unused):
            at = pl.ds(pl.multiple_of(i * 16, 16), 16)
            total = self.part[h.a, h.c, at].astype(F32) + self.near[0, at].astype(F32)
            for o in range(1, h.chain):
                total = total + self.far[o, at].astype(F32)
            out[at] = total
            return unused

        lax.fori_loop(0, rows // 16, add, 0)


def fold_offsets(here):
    return chain_offsets(here) + [dict(c=1)]


def fourth_kernel(part_ref, gr_ref, out_ref, gr_out, near, half, far, send, recv, gsend, grecv):
    h = Here()
    greet(h, chain_offsets(h) + block_offsets(h))
    wire = Wire(send, recv)
    fold = Fold(h, wire, part_ref, near, half, far)
    fold.start()
    slot = h.y * h.mid + h.b

    def chunk_copy(b, c):
        device = h.to(b=b, c=c)
        device["dp"] = h.c
        return pltpu.make_async_remote_copy(
            src_ref=gr_ref.at[h.b ^ b, h.c ^ c],
            dst_ref=gr_out.at[slot],
            send_sem=gsend.at[b * h.cores + c],
            recv_sem=grecv.at[slot],
            device_id=device,
            device_id_type=pl.DeviceIdType.MESH,
        )

    far_copies = [chunk_copy(b, c) for b in range(h.mid) for c in range(h.cores) if b or c]
    for copy in far_copies:
        copy.start()

    @pl.when(h.c == h.y)
    def _():
        pltpu.make_async_copy(gr_ref.at[h.b, h.c], gr_out.at[slot], grecv.at[slot]).start()

    @pl.when(h.c != h.y)
    def _():
        chunk_copy(0, 0).start()

    fold.pass_on()
    fold.finish(out_ref)
    for i in range(h.dp * h.mid):
        pltpu.make_async_copy(gr_out.at[i], gr_out.at[i], grecv.at[i]).wait()
    wire.drain()
    for copy in far_copies:
        copy.wait_send()

    @pl.when(h.c != h.y)
    def _():
        chunk_copy(0, 0).wait_send()


def fold_feed(part, gr, sizes):
    dp, chain, mid, cores = sizes
    return call(
        fourth_kernel,
        (
            jax.ShapeDtypeStruct(part.shape[2:], F32),
            jax.ShapeDtypeStruct((dp * mid,) + gr.shape[2:], BF),
        ),
        (part, gr),
        Fold.scratch(part)
        + wires(Fold.copies(chain))
        + [pltpu.SemaphoreType.DMA((mid * cores,)), pltpu.SemaphoreType.DMA((dp * mid,))],
        4,
        (VMEM, ANY),
        [VMEM, ANY],
    )


def fifth_kernel(
    q_ref, do_ref, lse_ref, delta_ref, kv_ref, part_ref, ge_ref,
    dq_ref, dkv_ref, out_ref, ge_out,
    made, got, near, half, far, send, recv, ksend, krecv,
):
    h = Here()
    span = kv_ref.shape[2]
    blocks = kv_ref.shape[0]
    greet(
        h,
        [
            dict(a=a, b=b, c=c)
            for a in range(h.chain)
            for b in range(h.mid)
            for c in range(h.cores)
            if a or b or c
        ]
        + [dict(y=y, b=b) for y, b in h.plane() if y],
    )
    wire = Wire(send, recv)
    fold = Fold(h, wire, part_ref, near, half, far)
    fold.start()
    sheets = []
    for i, (y, b) in enumerate(h.plane()):
        for a in range(h.chain):
            sheets.append(
                wire.push(ge_ref.at[h.y ^ y, a, h.b ^ b], ge_out.at[i, a], h.to(y=y, b=b))
            )
    fold.pass_on()

    last = h.rank // 2

    def visit(pair, hide):
        def head(g, unused):
            query, dout = q_ref[g], do_ref[g]
            keys = kv_ref[pl.ds(2 * pair, 2), g].reshape(2 * span, WIDE)
            probs = jnp.exp(mm(keys, query, NT) - lse_ref[g])
            if hide:
                probs = masked(probs, pair, h.rank, span)
            slope = probs * (mm(keys, dout, NT) - delta_ref[g])
            slope = slope.astype(BF)
            both = mm(slope, query, NN) + mm(probs.astype(BF), dout, NN)
            made[pl.ds(2 * pair, 2), g] = both.astype(BF).reshape(2, span, WIDE)
            add = mm(keys, slope, TN)[:HD]
            if hide:
                dq_ref[g] = add
            else:
                dq_ref[g] += add
            return unused

        lax.fori_loop(0, KV_HEADS, head, 0)

    def block_copy(o):
        peer = h.rank ^ o
        c, b, a = o % h.cores, (o // h.cores) % h.mid, o // (h.cores * h.mid)
        return pltpu.make_async_remote_copy(
            src_ref=made.at[peer],
            dst_ref=got.at[o],
            send_sem=ksend.at[o],
            recv_sem=krecv.at[o],
            device_id=h.to(a=a, b=b, c=c),
            device_id_type=pl.DeviceIdType.MESH,
        )

    visit(last, True)

    def step(pair, unused):
        visit(pair, False)
        return unused

    lax.fori_loop(0, last, step, 0)
    for o in range(1, blocks):

        @pl.when((h.rank ^ o) < h.rank)
        def _():
            block_copy(o).start()

    fold.finish(out_ref)
    dkv_ref[...] = made[h.rank].astype(F32)
    for o in range(1, blocks):

        @pl.when((h.rank ^ o) > h.rank)
        def _():
            block_copy(o).wait_recv()
            dkv_ref[...] += got[o].astype(F32)

        @pl.when((h.rank ^ o) < h.rank)
        def _():
            block_copy(o).wait_send()

    for copy in sheets:
        copy.wait_recv()
    wire.drain()


def attend_backward(query, dout, lse, delta, kv, part, ge, sizes):
    dp, chain, mid, cores = sizes
    blocks = chain * mid * cores
    rows = query.shape[1]
    others = dp * mid - 1
    return call(
        fifth_kernel,
        (
            jax.ShapeDtypeStruct((KV_HEADS, HD, rows), F32),
            jax.ShapeDtypeStruct(kv.shape[1:], F32),
            jax.ShapeDtypeStruct(part.shape[2:], F32),
            jax.ShapeDtypeStruct((others, chain) + ge.shape[3:], BF),
        ),
        (query, dout, lse, delta, kv, part, ge),
        [pltpu.VMEM(kv.shape, BF), pltpu.VMEM(kv.shape, BF)]
        + Fold.scratch(part)
        + wires(Fold.copies(chain) + others * chain)
        + wires(blocks),
        5,
        (VMEM, VMEM, VMEM, ANY),
        [VMEM, VMEM, VMEM, VMEM, VMEM, VMEM, ANY],
    )


class Scatter:
    def __init__(self, here, wire, grad, out, near, half, sheet, line, far, columns):
        self.here, self.wire, self.grad, self.out = here, wire, grad, out
        self.near, self.half, self.sheet, self.line, self.far = near, half, sheet, line, far
        self.columns = columns

    @staticmethod
    def copies(dp, chain, mid):
        return dp * mid + (dp * mid - 1) + (chain - 1)

    @staticmethod
    def scratch(grad):
        dp, chain, mid, cores, rows, width = grad.shape
        return [
            pltpu.VMEM((dp * mid, chain, rows, width), BF),
            pltpu.VMEM((dp * mid, chain, rows, width), BF),
            pltpu.VMEM((dp * mid, chain, rows, width), BF),
            pltpu.VMEM((chain, rows, width), BF),
            pltpu.VMEM((chain, rows, width), BF),
        ]

    def order(self):
        return self.here.plane() + [(0, 0)]

    def start(self):
        h = self.here
        self.swap = [
            self.wire.push(
                self.grad.at[h.y ^ y, :, h.b ^ b, h.c ^ 1, :, self.columns],
                self.near.at[i, :, :, self.columns],
                h.to(c=1),
            )
            for i, (y, b) in enumerate(self.order())
        ]

    def over_plane(self):
        h = self.here
        self.sent = []
        for i, (y, b) in enumerate(self.order()):
            self.swap[i].wait_recv()

            def add(a, unused):
                total = (
                    self.grad[h.y ^ y, a, h.b ^ b, h.c, :, self.columns].astype(F32)
                    + self.near[i, a, :, self.columns].astype(F32)
                )
                self.half[i, a, :, self.columns] = total.astype(BF)
                return unused

            lax.fori_loop(0, h.chain, add, 0)
            if y or b:
                self.sent.append(
                    self.wire.push(
                        self.half.at[i, :, :, self.columns],
                        self.sheet.at[i, :, :, self.columns],
                        h.to(y=y, b=b),
                    )
                )

    def over_chain(self):
        h = self.here
        own = len(self.order()) - 1
        for copy in self.sent:
            copy.wait_recv()
        self.last = []
        for o in list(range(1, h.chain)) + [0]:
            total = self.half[own, h.a ^ o, :, self.columns].astype(F32)
            for i in range(own):
                total = total + self.sheet[i, h.a ^ o, :, self.columns].astype(F32)
            if o:
                self.line[o, :, self.columns] = total.astype(BF)
                self.last.append(
                    self.wire.push(
                        self.line.at[o, :, self.columns],
                        self.far.at[o, :, self.columns],
                        h.to(a=o),
                    )
                )
            else:
                self.out[:, self.columns] = total

    def finish(self):
        h = self.here
        for copy in self.last:
            copy.wait_recv()
        total = self.out[:, self.columns]
        for o in range(1, h.chain):
            total = total + self.far[o, :, self.columns].astype(F32)
        self.out[:, self.columns] = total


def sixth_kernel(
    gi_ref, go_ref, ge_ref, gi_out, go_out, ge_out,
    n1, h1, s1, l1, f1, n2, h2, s2, l2, f2, send, recv, local,
):
    h = Here()
    greet(
        h,
        [dict(a=a, c=c) for a in range(h.chain) for c in range(h.cores) if a or c]
        + plane_offsets(h),
    )
    wire = Wire(send, recv)
    width = FF // (h.chain * h.cores)
    jobs = [
        Scatter(h, wire, gi_ref, gi_out, n1, h1, s1, l1, f1, columns)
        for columns in (pl.ds(0, gi_ref.shape[-1] // 2), pl.ds(gi_ref.shape[-1] // 2, gi_ref.shape[-1] // 2))
    ] + [Scatter(h, wire, go_ref, go_out, n2, h2, s2, l2, f2, pl.ds(0, go_ref.shape[-1]))]
    for job in jobs:
        job.start()
    kept, swaps = [], []
    chunk = h.c * h.chain + h.a
    for a in range(h.chain):
        for c in range(h.cores):
            for part in range(2):
                source = ge_ref.at[h.a ^ a, h.c ^ c, :, pl.ds(part * width, width)]
                spot = ge_out.at[:, chunk_columns(chunk, part, width)]
                if a or c:
                    swaps.append(wire.push(source, spot, h.to(a=a, c=c)))
                else:
                    copy = pltpu.make_async_copy(source, spot, local.at[part])
                    copy.start()
                    kept.append(copy)
    jobs[0].over_plane()
    jobs[1].over_plane()
    jobs[2].over_plane()
    for job in jobs:
        job.over_chain()
    for job in jobs:
        job.finish()
    for copy in swaps:
        copy.wait_recv()
    wire.drain()
    for copy in kept:
        copy.wait()


def scatter_projections(gi, go, ge, sizes):
    dp, chain, mid, cores = sizes
    count = 3 * Scatter.copies(dp, chain, mid) + 2 * (chain * cores - 1)
    return call(
        sixth_kernel,
        (
            jax.ShapeDtypeStruct(gi.shape[4:], F32),
            jax.ShapeDtypeStruct(go.shape[4:], F32),
            jax.ShapeDtypeStruct((ge.shape[2], 2 * FF), BF),
        ),
        (gi, go, ge),
        Scatter.scratch(gi)
        + Scatter.scratch(go)
        + wires(count)
        + [pltpu.SemaphoreType.DMA((2,))],
        6,
        (VMEM, VMEM, ANY),
        [VMEM, VMEM, ANY],
    )


def seventh_kernel(x_ref, out_ref, got, send, recv):
    h = Here()
    offsets = [
        dict(y=y, a=a, b=b, c=c)
        for y in range(h.dp)
        for a in range(h.chain)
        for b in range(h.mid)
        for c in range(h.cores)
        if y or a or b or c
    ]
    greet(h, offsets)
    wire = Wire(send, recv)
    copies = [wire.push(x_ref, got.at[h.shard], h.to(**offset)) for offset in offsets]
    got[h.shard] = x_ref[...]
    for copy in copies:
        copy.wait_recv()
    out_ref[...] = jnp.sum(got[...], axis=0)
    wire.drain()


def total_of(x, sizes):
    count = math.prod(sizes)
    return call(
        seventh_kernel,
        jax.ShapeDtypeStruct(x.shape, F32),
        (x,),
        [pltpu.VMEM((count,) + x.shape, F32)] + wires(count),
        7,
        VMEM,
        [VMEM],
    )


def rms_normed(values, gains):
    mean_square = jnp.mean(values * values, axis=-1, keepdims=True)
    return values * lax.rsqrt(mean_square + EPSILON) * gains


def rotary(values, positions):
    half_width = values.shape[-1] // 2
    frequency = THETA ** (-2.0 * jnp.arange(half_width).astype(F32) / values.shape[-1])
    angles = positions.astype(F32)[:, None] * frequency[None, :]
    cosine = jnp.cos(angles)[:, None, :]
    sine_rows = jnp.sin(angles)[:, None, :]
    front_half = values[..., :half_width]
    back_half = values[..., half_width:]
    return jnp.concatenate(
        [front_half * cosine - back_half * sine_rows, back_half * cosine + front_half * sine_rows],
        axis=-1,
    )


def prepare(projected, head_gains, positions):
    row_count = projected.shape[0]
    queries = projected[:, : HEADS * HD].reshape(row_count, HEADS, HD)
    key_rows = projected[:, HEADS * HD : (HEADS + KV_HEADS) * HD].reshape(row_count, KV_HEADS, HD)
    value_rows = projected[:, (HEADS + KV_HEADS) * HD :].reshape(row_count, KV_HEADS, HD)
    queries = rotary(rms_normed(queries, head_gains[0]), positions)
    key_rows = rotary(rms_normed(key_rows, head_gains[1]), positions)
    return (queries, key_rows, value_rows)


def by_group(values):
    rows = values.shape[0]
    values = values.reshape(rows, KV_HEADS, GROUP, HD).transpose(1, 2, 0, 3)
    return values.reshape(KV_HEADS, GROUP * rows, HD)


def by_row(values, rows):
    values = values.reshape(KV_HEADS, HD, GROUP, rows).transpose(3, 0, 2, 1)
    return values.reshape(rows, HEADS * HD)


def on_device(
    sizes,
    tokens,
    cotangent,
    norm_gains,
    head_gains,
    input_weight,
    output_weight,
    expand_weight,
    reduce_weight,
    norm_moment,
    head_moment,
    input_moment,
    output_moment,
    expand_moment,
    reduce_moment,
    learn_rate,
):
    dp, chain, mid, cores = sizes
    seq_count, rows, model_width = tokens.shape
    assert seq_count == 1
    place = (lax.axis_index("a") * mid + lax.axis_index("b")) * cores + lax.axis_index("c")
    positions = place * rows + jnp.arange(rows, dtype=jnp.int32)
    score_scale = 1.0 / math.sqrt(HD)
    upstream_low = cotangent.reshape(rows, model_width)

    full_input, e1 = gather_first(input_weight.astype(BF), expand_weight.astype(BF), sizes)
    full_input = full_input.reshape(model_width, -1)
    input_rows = tokens.reshape(rows, model_width).astype(F32)
    normed_one, norm_one_pull = jax.vjp(rms_normed, input_rows, norm_gains[0])
    normed_one = normed_one.astype(BF)
    projected = jnp.dot(normed_one, full_input, preferred_element_type=F32)

    def prepare_here(projected_rows, gains):
        return prepare(projected_rows, gains, positions)

    (queries, key_rows, value_rows), prepare_pull = jax.vjp(prepare_here, projected, head_gains)
    query_low = by_group((queries.astype(BF) * score_scale).reshape(rows, HEADS * HD))
    query_wide = jnp.pad(query_low, ((0, 0), (0, 0), (0, HD)))
    kv_low = jnp.concatenate([key_rows, value_rows], axis=-1).astype(BF).transpose(1, 0, 2)

    attended_cols, log_mass, kv_all, full_output, cot_all = attend_forward(
        query_wide, kv_low, output_weight.astype(BF), upstream_low, sizes
    )
    full_output = full_output.reshape(-1, model_width)
    attended = by_row(attended_cols, rows)
    attended_low = attended.astype(BF)
    branch = jnp.dot(attended_low, full_output, preferred_element_type=F32)
    residual = input_rows + branch
    normed_two, norm_two_pull = jax.vjp(rms_normed, residual, norm_gains[1])
    normed_two = normed_two.astype(BF)

    n_all, ex_all, rd_all = gather_feed(normed_two, e1, reduce_weight.astype(BF), sizes)
    n_all = n_all.reshape(-1, model_width)
    cot_all = cot_all.reshape(-1, model_width)
    ex_all = ex_all.reshape(model_width, -1)
    rd_all = rd_all.reshape(-1, model_width)
    part_width = rd_all.shape[0]
    expanded = jnp.dot(n_all, ex_all, preferred_element_type=F32)
    gate_value = expanded[:, :part_width]
    up_value = expanded[:, part_width:]
    sigmoid = jax.nn.sigmoid(gate_value)
    activated = gate_value * sigmoid
    slope = sigmoid * (1.0 + gate_value * (1.0 - sigmoid))
    hidden = (activated * up_value).astype(BF)
    hidden_grad = jnp.einsum("rd,fd->rf", cot_all, rd_all, preferred_element_type=F32)
    expand_grad = jnp.concatenate(
        [hidden_grad * up_value * slope, hidden_grad * activated], axis=1
    ).astype(BF)
    back_part = jnp.einsum("rf,df->rd", expand_grad, ex_all, preferred_element_type=F32).astype(BF)
    grad_reduce = jnp.einsum("rf,rd->fd", hidden, cot_all, preferred_element_type=F32).astype(BF)
    normed_two_grad, reduce_got = fold_feed(
        back_part.reshape(chain, cores, rows, model_width),
        grad_reduce.reshape(mid, cores, -1, model_width),
        sizes,
    )
    out_part = jnp.dot(hidden, rd_all, preferred_element_type=F32).astype(BF)
    grad_expand = jnp.einsum("rd,rf->df", n_all, expand_grad, preferred_element_type=F32).astype(BF)

    residual_part, gain_two_grad = norm_two_pull(normed_two_grad)
    residual_grad = upstream_low.astype(F32) + residual_part
    branch_grad = residual_grad.astype(BF)
    grad_output = jnp.einsum("rh,rd->hd", attended_low, branch_grad, preferred_element_type=F32)
    attended_grad = jnp.einsum(
        "rd,hd->rh", branch_grad, full_output, preferred_element_type=F32
    ).astype(BF)
    row_delta = jnp.sum(
        (attended_grad.astype(F32) * attended).reshape(rows, KV_HEADS, GROUP, HD), axis=-1
    )
    row_delta = row_delta.transpose(1, 2, 0).reshape(KV_HEADS, 1, GROUP * rows)
    dout_wide = jnp.pad(by_group(attended_grad), ((0, 0), (0, 0), (HD, 0)))
    grad_expand = grad_expand.reshape(dp, chain, mid, cores, -1, grad_expand.shape[1])
    query_cols, kv_grad, result, expand_got = attend_backward(
        query_wide,
        dout_wide,
        log_mass,
        row_delta,
        kv_all,
        out_part.reshape(chain, cores, rows, model_width),
        grad_expand,
        sizes,
    )
    query_grads = by_row(query_cols, rows) * score_scale
    kv_grad = kv_grad.transpose(1, 0, 2)
    projected_grad, head_grads = prepare_pull(
        (query_grads.reshape(rows, HEADS, HD), kv_grad[..., :HD], kv_grad[..., HD:])
    )
    projected_low = projected_grad.astype(BF)
    grad_input = jnp.einsum("rd,rc->dc", normed_one, projected_low, preferred_element_type=F32)
    normed_one_grad = jnp.einsum(
        "rc,dc->rd", projected_low, full_input, preferred_element_type=F32
    )
    input_part, gain_one_grad = norm_one_pull(normed_one_grad)
    token_low = (residual_grad + input_part).astype(BF).reshape(tokens.shape)
    layer_out = (residual + result).astype(BF).reshape(tokens.shape)

    y_here, b_here = lax.axis_index("dp"), lax.axis_index("b")
    own_expand = lax.dynamic_index_in_dim(grad_expand, y_here, 0, keepdims=False)
    own_expand = lax.dynamic_index_in_dim(own_expand, b_here, 1, keepdims=False)
    sum_expand = own_expand.astype(F32) + jnp.sum(expand_got.astype(F32), axis=0)
    shard_reduce = jnp.sum(reduce_got.astype(F32), axis=0)

    def sharded(grad):
        return grad.astype(BF).reshape(dp, chain, mid, cores, -1, grad.shape[1])

    shard_input, shard_output, shard_expand = scatter_projections(
        sharded(grad_input), sharded(grad_output), sum_expand.astype(BF), sizes
    )
    shard_expand = shard_expand.astype(F32)
    squares_local = (
        jnp.sum(shard_input * shard_input)
        + jnp.sum(shard_output * shard_output)
        + jnp.sum(shard_expand * shard_expand)
        + jnp.sum(shard_reduce * shard_reduce)
    )
    gain_count = norm_gains.size
    head_count = head_gains.size
    packed = jnp.concatenate(
        [
            gain_one_grad,
            gain_two_grad,
            head_grads.reshape(-1),
            jnp.full((128,), squares_local, F32),
        ]
    ).reshape(-1, 128)
    packed = jnp.pad(packed, ((0, -packed.shape[0] % 8), (0, 0)))
    totals = total_of(packed, sizes).reshape(-1)
    gain_totals = totals[:gain_count].reshape(norm_gains.shape)
    head_totals = totals[gain_count : gain_count + head_count].reshape(head_gains.shape)
    square_total = totals[gain_count + head_count]
    grad_norm = jnp.sqrt(
        square_total + jnp.sum(gain_totals * gain_totals) + jnp.sum(head_totals * head_totals)
    )
    clip_limit = math.sqrt(NPARAM)
    factor = clip_limit / jnp.maximum(grad_norm, clip_limit)

    def advance(weight, moment, gradient):
        new_moment = MOMENTUM * moment + factor * gradient
        return (new_moment, weight - learn_rate * new_moment)

    moment_norms, next_norms = advance(norm_gains, norm_moment, gain_totals)
    moment_heads, next_heads = advance(head_gains, head_moment, head_totals)
    moment_input, next_input = advance(input_weight, input_moment, shard_input)
    moment_output, next_output = advance(output_weight, output_moment, shard_output)
    moment_expand, next_expand = advance(expand_weight, expand_moment, shard_expand)
    moment_reduce, next_reduce = advance(reduce_weight, reduce_moment, shard_reduce)
    return (
        layer_out,
        token_low,
        grad_norm,
        moment_norms,
        moment_heads,
        moment_input,
        moment_output,
        moment_expand,
        moment_reduce,
        next_norms,
        next_heads,
        next_input,
        next_output,
        next_expand,
        next_reduce,
    )


def solution(mesh):
    dp, ctx = mesh.shape["dp"], mesh.shape["ctx"]
    sizes = (dp, CHAIN, ctx // (CHAIN * CORES), CORES)
    assert dp == CORES
    grid = Mesh(mesh.devices.reshape(sizes), AXES)
    rows = P("dp", ("a", "b", "c"), None)
    shard = P(AXES, None)
    in_specs = (rows, rows, P(), P(), shard, shard, shard, shard)
    in_specs += (P(), P(), shard, shard, shard, shard, P())
    out_specs = (rows, rows, P(), P(), P(), shard, shard, shard, shard)
    out_specs += (P(), P(), shard, shard, shard, shard)
    return jax.shard_map(
        functools.partial(on_device, sizes),
        mesh=grid,
        in_specs=in_specs,
        out_specs=out_specs,
        check_vma=False,
    )
```

```python
import functools
import math

import jax
import jax.numpy as jnp
from jax import lax
from jax.experimental import pallas as pl
from jax.experimental.pallas import tpu as pltpu
from jax.sharding import Mesh
from jax.sharding import PartitionSpec as P

HEADS = 24
KV_HEADS = 6
HD = 64
FF = 5120
GROUP = 4
NPARAM = 39325824


EPSILON = 1e-06
THETA = 10000.0
MOMENTUM = 0.5

BF = jnp.bfloat16
F32 = jnp.float32
WIDE = 2 * HD
CHAIN = 4
CORES = 2
AXES = ("dp", "a", "b", "c")
ANY = pl.BlockSpec(memory_space=pl.ANY)
VMEM = pl.BlockSpec(memory_space=pltpu.VMEM)
NT = (((1,), (1,)), ((), ()))
TN = (((0,), (0,)), ((), ()))
NN = (((1,), (0,)), ((), ()))


def mm(left, right, dims):
    return lax.dot_general(left, right, dims, preferred_element_type=F32)


class Here:
    def __init__(self):
        self.y, self.a, self.b, self.c = (lax.axis_index(name) for name in AXES)
        self.dp, self.chain, self.mid, self.cores = (lax.axis_size(name) for name in AXES)
        self.rank = (self.a * self.mid + self.b) * self.cores + self.c
        self.shard = self.y * (self.chain * self.mid * self.cores) + self.rank

    def to(self, y=0, a=0, b=0, c=0):
        out = {}
        for name, mine, offset in zip(AXES, (self.y, self.a, self.b, self.c), (y, a, b, c)):
            out[name] = mine ^ offset if offset else mine
        return out

    def plane(self):
        return [
            (y, b) for y in range(self.dp) for b in range(self.mid) if y or b
        ]


def greet(here, offsets):
    barrier = pltpu.get_barrier_semaphore()
    for offset in offsets:
        pl.semaphore_signal(
            barrier, inc=1, device_id=here.to(**offset), device_id_type=pl.DeviceIdType.MESH
        )
    pl.semaphore_wait(barrier, len(offsets))


class Wire:
    def __init__(self, send, recv):
        self.send, self.recv, self.made = send, recv, []

    def push(self, source, target, device):
        k = len(self.made)
        copy = pltpu.make_async_remote_copy(
            src_ref=source,
            dst_ref=target,
            send_sem=self.send.at[k],
            recv_sem=self.recv.at[k],
            device_id=device,
            device_id_type=pl.DeviceIdType.MESH,
        )
        copy.start()
        self.made.append(copy)
        return copy

    def drain(self):
        for copy in self.made:
            copy.wait_send()


def wires(count):
    return [pltpu.SemaphoreType.DMA((count,)), pltpu.SemaphoreType.DMA((count,))]


def chain_offsets(here):
    return [dict(a=o) for o in range(1, here.chain)]


def plane_offsets(here):
    return [dict(y=y, b=b) for y, b in here.plane()]


def block_offsets(here):
    return [
        dict(y=y, b=b, c=c)
        for y in range(here.dp)
        for b in range(here.mid)
        for c in range(here.cores)
        if y or b or c
    ]


def planar(here, number):
    pair = [("b", here.mid), ("y", here.dp)]
    return pair if number % 2 == 0 else pair[::-1]


class Sheet:
    def __init__(self, here, wire, spot):
        self.here, self.wire, self.spot = here, wire, spot
        self.first, self.second = {}, {}

    def start(self, number, source):
        h = self.here
        (one, n_one), (two, n_two) = planar(h, number)
        slot = self.spot(number, 0, 0)
        for k in range(1, n_one):
            self.first[number, k] = self.wire.push(source, slot, h.to(**{one: k}))
        for s in range(1, n_two):
            self.second[number, 0, s] = self.wire.push(source, slot, h.to(**{two: s}))

    def relay(self, number, landed=None):
        h = self.here
        (one, n_one), (two, n_two) = planar(h, number)
        for k in range(1, n_one):
            self.first[number, k].wait_recv()
            slot = self.spot(number, *self.place(one, k))
            for s in range(1, n_two):
                self.second[number, k, s] = self.wire.push(slot, slot, h.to(**{two: s}))
            if landed:
                landed(slot)

    def finish(self, number, landed=None):
        h = self.here
        (one, n_one), (two, n_two) = planar(h, number)
        for k in range(n_one):
            for s in range(1, n_two):
                self.second[number, k, s].wait_recv()
                if landed:
                    y1, b1 = self.place(one, k)
                    y2, b2 = self.place(two, s)
                    landed(self.spot(number, y1 + y2, b1 + b2))

    @staticmethod
    def place(name, offset):
        return (offset, 0) if name == "y" else (0, offset)


class Gather:
    def __init__(self, here, wire, shard, full):
        self.here, self.wire, self.shard = here, wire, shard
        self.core = []

        def spot(number, y, b):
            return full.at[here.y ^ y, here.a ^ number, here.b ^ b, here.c]

        self.sheet = Sheet(here, wire, spot)

    @staticmethod
    def copies(dp, chain, mid):
        return (chain - 1) + (dp * mid - 1) * chain + dp * chain * mid

    def landed(self, slot):
        self.core.append(self.wire.push(slot, slot, self.here.to(c=1)))

    def start(self):
        h = self.here
        slot = self.sheet.spot(0, 0, 0)
        self.chain = {
            o: self.wire.push(self.shard, slot, h.to(a=o)) for o in range(1, h.chain)
        }
        self.sheet.start(0, self.shard)
        self.core.append(self.wire.push(self.shard, slot, h.to(c=1)))

    def relay_chain(self):
        for o in range(1, self.here.chain):
            self.chain[o].wait_recv()
            slot = self.sheet.spot(o, 0, 0)
            self.sheet.start(o, slot)
            self.landed(slot)

    def relay_plane(self):
        for o in range(self.here.chain):
            self.sheet.relay(o, self.landed)

    def finish(self):
        for o in range(self.here.chain):
            self.sheet.finish(o, self.landed)
        for copy in self.core:
            copy.wait_recv()


class Line:
    def __init__(self, here, block, full, sems):
        self.here, self.block, self.full = here, block, full
        self.send, self.recv, self.csend, self.crecv = sems

    @staticmethod
    def scratch(chain):
        return [pltpu.SemaphoreType.DMA((n,)) for n in (2 * chain, chain, chain, chain)]

    def along(self, source, owner, target, number):
        return pltpu.make_async_remote_copy(
            src_ref=source,
            dst_ref=self.full.at[owner, self.here.c],
            send_sem=self.send.at[number],
            recv_sem=self.recv.at[owner],
            device_id={"a": target},
            device_id_type=pl.DeviceIdType.MESH,
        )

    def across(self, source, owner):
        return pltpu.make_async_remote_copy(
            src_ref=source,
            dst_ref=self.full.at[owner, self.here.c],
            send_sem=self.csend.at[owner],
            recv_sem=self.crecv.at[owner],
            device_id=self.here.to(c=1),
            device_id_type=pl.DeviceIdType.MESH,
        )

    def start(self):
        h = self.here

        @pl.when(h.a < h.chain - 1)
        def _():
            self.along(self.block, h.a, h.a + 1, 0).start()

        @pl.when(h.a > 0)
        def _():
            self.along(self.block, h.a, h.a - 1, 1).start()

        self.across(self.block, h.a).start()

    def step(self, s):
        h = self.here

        @pl.when(h.a - s >= 0)
        def _():
            owner = h.a - s
            spot = self.full.at[owner, h.c]
            self.along(spot, owner, h.a, 0).wait_recv()

            @pl.when(h.a < h.chain - 1)
            def _():
                self.along(spot, owner, h.a + 1, 2 * s).start()

            self.across(spot, owner).start()

        @pl.when(h.a + s < h.chain)
        def _():
            owner = h.a + s
            spot = self.full.at[owner, h.c]
            self.along(spot, owner, h.a, 0).wait_recv()

            @pl.when(h.a > 0)
            def _():
                self.along(spot, owner, h.a - 1, 2 * s + 1).start()

            self.across(spot, owner).start()

    def finish(self):
        h = self.here
        for s in range(h.chain):

            @pl.when((h.a - s >= 0) & (h.a < h.chain - 1))
            def _():
                self.along(self.block, h.a, h.a, 2 * s).wait_send()

            @pl.when((h.a + s < h.chain) & (h.a > 0))
            def _():
                self.along(self.block, h.a, h.a, 2 * s + 1).wait_send()

        for owner in range(h.chain):
            self.across(self.block, owner).wait_recv()
            self.across(self.block, owner).wait_send()


def call(body, outs, ins, scratch, ident, out_specs, in_specs, aliases=()):
    return pl.pallas_call(
        body,
        out_shape=outs,
        in_specs=in_specs,
        out_specs=out_specs,
        scratch_shapes=scratch,
        input_output_aliases=dict(aliases),
        compiler_params=pltpu.CompilerParams(collective_id=ident, has_side_effects=True),
    )(*ins)


def chunk_columns(chunk, part, width):
    start = part * FF + chunk * width
    return pl.ds(pl.multiple_of(start, 128), width)


def first_kernel(win_ref, ex_ref, win_out, e1_out, send, recv, local):
    h = Here()
    width = FF // (h.chain * h.cores)
    greet(h, [dict(a=a, c=c) for a in range(h.chain) for c in range(h.cores) if a or c] + plane_offsets(h))
    wire = Wire(send, recv)
    own = pltpu.make_async_copy(win_ref, win_out.at[h.y, h.a, h.b, h.c], local.at[0])
    own.start()
    gather = Gather(h, wire, win_ref, win_out)
    gather.start()
    kept = []
    for part in range(2):
        mine = ex_ref.at[:, chunk_columns(h.c * h.chain + h.a, part, width)]
        spot = e1_out.at[h.a, h.c, :, pl.ds(part * width, width)]
        copy = pltpu.make_async_copy(mine, spot, local.at[1 + part])
        copy.start()
        kept.append(copy)
    swaps = []
    for a in range(h.chain):
        for c in range(h.cores):
            if not (a or c):
                continue
            for part in range(2):
                chunk = (h.c ^ c) * h.chain + (h.a ^ a)
                source = ex_ref.at[:, chunk_columns(chunk, part, width)]
                spot = e1_out.at[h.a, h.c, :, pl.ds(part * width, width)]
                swaps.append(wire.push(source, spot, h.to(a=a, c=c)))
    gather.relay_chain()
    gather.relay_plane()
    gather.finish()
    for copy in swaps:
        copy.wait_recv()
    wire.drain()
    own.wait()
    for copy in kept:
        copy.wait()


def gather_first(win, ex, sizes):
    dp, chain, mid, cores = sizes
    rows = win.shape[0]
    width = 2 * FF // (chain * cores)
    count = Gather.copies(dp, chain, mid) + 2 * (chain * cores - 1)
    return call(
        first_kernel,
        (
            jax.ShapeDtypeStruct((dp, chain, mid, cores) + win.shape, BF),
            jax.ShapeDtypeStruct((chain, cores, rows, width), BF),
        ),
        (win, ex),
        wires(count) + [pltpu.SemaphoreType.DMA((3,))],
        1,
        (ANY, ANY),
        [ANY, ANY],
    )


def masked(values, pair, rank, span):
    key_pos = pair * (2 * span) + lax.broadcasted_iota(jnp.int32, values.shape, 0)
    query_pos = rank * span + lax.rem(lax.broadcasted_iota(jnp.int32, values.shape, 1), span)
    return jnp.where(key_pos <= query_pos, values, 0.0)


def expand_sheet(here, wire, ex_out):
    def spot(number, y, b):
        return ex_out.at[here.y ^ y, number, here.b ^ b]

    return Sheet(here, wire, spot)


EARLY = 3


def second_kernel(
    q_ref, kv_ref, wout_ref, cot_ref, e1_ref,
    o_ref, lse_ref, kv_out, wout_out, cot_out, ex_out,
    kv_all, send, recv, lsend, lrecv, lcsend, lcrecv, local,
):
    h = Here()
    span = kv_ref.shape[1]
    greet(h, chain_offsets(h) + plane_offsets(h) + [dict(c=1)])
    wire = Wire(send, recv)
    own_out = pltpu.make_async_copy(wout_ref, wout_out.at[h.y, h.a, h.b, h.c], local.at[0])
    own_out.start()
    own_cot = pltpu.make_async_copy(cot_ref, cot_out.at[h.a, h.c], local.at[1])
    own_cot.start()

    def block(a, b, c):
        return kv_all.at[((h.a ^ a) * h.mid + (h.b ^ b)) * h.cores + (h.c ^ c)]

    mine = block(0, 0, 0)
    mine[...] = kv_ref[...]
    core = []
    chain = {o: wire.push(kv_ref, mine, h.to(a=o)) for o in range(1, h.chain)}
    side = {(0, b): wire.push(kv_ref, mine, h.to(b=b)) for b in range(1, h.mid)}
    core.append(wire.push(kv_ref, mine, h.to(c=1)))
    gather = Gather(h, wire, wout_ref, wout_out)
    gather.start()
    cots = Line(h, cot_ref, cot_out, (lsend, lrecv, lcsend, lcrecv))
    cots.start()
    for o in range(1, h.chain):
        chain[o].wait_recv()
        spot = block(o, 0, 0)
        for b in range(1, h.mid):
            side[o, b] = wire.push(spot, spot, h.to(b=b))
        core.append(wire.push(spot, spot, h.to(c=1)))
    sheet = expand_sheet(h, wire, ex_out)
    kept = []
    for a in range(EARLY):
        sheet.start(a, e1_ref.at[a])
        copy = pltpu.make_async_copy(e1_ref.at[a], ex_out.at[h.y, a, h.b], local.at[3 + a])
        copy.start()
        kept.append(copy)
    for o in range(h.chain):
        for b in range(1, h.mid):
            side[o, b].wait_recv()
            spot = block(o, b, 0)
            core.append(wire.push(spot, spot, h.to(c=1)))
    for copy in core:
        copy.wait_recv()
    store = pltpu.make_async_copy(kv_all, kv_out, local.at[2])
    store.start()

    last = h.rank // 2

    def head(g, unused):
        query = q_ref[g]

        def visit(pair, hide):
            keys = kv_all[pl.ds(2 * pair, 2), g].reshape(2 * span, WIDE)
            weights = jnp.exp(mm(keys, query, NT))
            if hide:
                weights = masked(weights, pair, h.rank, span)
            total = jnp.sum(weights, axis=0, keepdims=True)
            return total, mm(keys, weights.astype(BF), TN)[HD:]

        total, value = visit(last, True)
        lse_ref[g] = total
        o_ref[g] = value

        def step(pair, unused_inner):
            total, value = visit(pair, False)
            lse_ref[g] += total
            o_ref[g] += value
            return unused_inner

        lax.fori_loop(0, last, step, 0)
        o_ref[g] = o_ref[g] / lse_ref[g]
        lse_ref[g] = jnp.log(lse_ref[g])
        return unused

    lax.fori_loop(0, 2, head, 0)
    gather.relay_chain()
    cots.step(1)
    lax.fori_loop(2, 4, head, 0)
    sheet.relay(0)
    cots.step(2)
    lax.fori_loop(4, KV_HEADS, head, 0)
    for a in range(1, EARLY):
        sheet.relay(a)
    gather.relay_plane()
    cots.step(3)
    gather.finish()
    for a in range(EARLY):
        sheet.finish(a)
    cots.finish()
    wire.drain()
    own_out.wait()
    own_cot.wait()
    store.wait()
    for copy in kept:
        copy.wait()


def attend_forward(query, kv, wout, cot, e1, sizes):
    dp, chain, mid, cores = sizes
    assert chain == CHAIN
    blocks = chain * mid * cores
    rows = query.shape[1]
    count = (
        (chain - 1) + (mid - 1) * chain + chain * mid
        + Gather.copies(dp, chain, mid) + EARLY * (dp * mid - 1)
    )
    return call(
        second_kernel,
        (
            jax.ShapeDtypeStruct((KV_HEADS, HD, rows), F32),
            jax.ShapeDtypeStruct((KV_HEADS, 1, rows), F32),
            jax.ShapeDtypeStruct((blocks,) + kv.shape, BF),
            jax.ShapeDtypeStruct((dp, chain, mid, cores) + wout.shape, BF),
            jax.ShapeDtypeStruct((chain, cores) + cot.shape, BF),
            jax.ShapeDtypeStruct((dp, chain, mid) + e1.shape[1:], BF),
        ),
        (query, kv, wout, cot, e1),
        [pltpu.VMEM((blocks,) + kv.shape, BF)]
        + wires(count)
        + Line.scratch(chain)
        + [pltpu.SemaphoreType.DMA((3 + EARLY,))],
        2,
        (VMEM, VMEM, ANY, ANY, ANY, ANY),
        [VMEM, VMEM, ANY, ANY, ANY],
    )


def third_kernel(
    n_ref, e1_ref, rd_ref, ex_ref, n_out, rd_out, ex_out,
    send, recv, rsend, rrecv, lsend, lrecv, lcsend, lcrecv, local,
):
    h = Here()
    greet(h, chain_offsets(h) + block_offsets(h))
    wire = Wire(send, recv)
    rows = Line(h, n_ref, n_out, (lsend, lrecv, lcsend, lcrecv))
    rows.start()
    own = pltpu.make_async_copy(n_ref, n_out.at[h.a, h.c], local.at[0])
    own.start()
    sheet = expand_sheet(h, wire, ex_out)
    kept = []
    for a in range(EARLY, h.chain):
        sheet.start(a, e1_ref.at[a])
        copy = pltpu.make_async_copy(e1_ref.at[a], ex_out.at[h.y, a, h.b], local.at[1 + a])
        copy.start()
        kept.append(copy)
    slot = h.b * h.cores + h.c

    def reduce_copy(number, y, b):
        device = h.to(y=y, b=b)
        device["c"] = h.y
        return pltpu.make_async_remote_copy(
            src_ref=rd_ref,
            dst_ref=rd_out.at[h.b, h.c],
            send_sem=rsend.at[number],
            recv_sem=rrecv.at[slot],
            device_id=device,
            device_id_type=pl.DeviceIdType.MESH,
        )

    far = [reduce_copy(1 + i, y, b) for i, (y, b) in enumerate(h.plane())]
    for copy in far:
        copy.start()

    @pl.when(h.c == h.y)
    def _():
        pltpu.make_async_copy(rd_ref, rd_out.at[h.b, h.c], rrecv.at[slot]).start()

    @pl.when(h.c != h.y)
    def _():
        reduce_copy(0, 0, 0).start()

    rows.step(1)
    for a in range(EARLY, h.chain):
        sheet.relay(a)
    for s in range(2, h.chain):
        rows.step(s)
    for a in range(EARLY, h.chain):
        sheet.finish(a)
    for b in range(h.mid):
        for c in range(h.cores):
            spot = rd_out.at[b, c]
            pltpu.make_async_copy(spot, spot, rrecv.at[b * h.cores + c]).wait()
    rows.finish()
    wire.drain()
    for copy in far:
        copy.wait_send()

    @pl.when(h.c != h.y)
    def _():
        reduce_copy(0, 0, 0).wait_send()

    own.wait()
    for copy in kept:
        copy.wait()


def gather_feed(normed, e1, rd, ex, sizes):
    dp, chain, mid, cores = sizes
    count = (chain - EARLY) * (dp * mid - 1)
    return call(
        third_kernel,
        (
            jax.ShapeDtypeStruct((chain, cores) + normed.shape, BF),
            jax.ShapeDtypeStruct((mid, cores) + rd.shape, BF),
            jax.ShapeDtypeStruct(ex.shape, BF),
        ),
        (normed, e1, rd, ex),
        wires(count)
        + [pltpu.SemaphoreType.DMA((dp * mid,)), pltpu.SemaphoreType.DMA((mid * cores,))]
        + Line.scratch(chain)
        + [pltpu.SemaphoreType.DMA((1 + chain,))],
        3,
        (ANY, ANY, ANY),
        [ANY, ANY, ANY, ANY],
        aliases={3: 2},
    )


class Fold:
    def __init__(self, here, wire, part, near, far):
        self.here, self.wire, self.part = here, wire, part
        self.near, self.far = near, far

    @staticmethod
    def copies(chain):
        return chain + chain - 1

    @staticmethod
    def scratch(part):
        chain, cores, rows, width = part.shape
        return [pltpu.VMEM((chain, rows, width), BF) for _ in range(2)]

    def start(self):
        h = self.here
        self.swap = {
            o: self.wire.push(self.part.at[h.a ^ o, h.c ^ 1], self.near.at[o], h.to(c=1))
            for o in list(range(1, h.chain)) + [0]
        }

    def pass_on(self):
        h = self.here
        self.sent = {}
        rows = self.part.shape[2]
        for o in range(1, h.chain):
            self.swap[o].wait_recv()

            def add(i, unused):
                at = pl.ds(pl.multiple_of(i * 16, 16), 16)
                both = self.part[h.a ^ o, h.c, at].astype(F32) + self.near[o, at].astype(F32)
                self.near[o, at] = both.astype(BF)
                return unused

            lax.fori_loop(0, rows // 16, add, 0)
            self.sent[o] = self.wire.push(self.near.at[o], self.far.at[o], h.to(a=o))
        self.swap[0].wait_recv()

    def finish(self, out):
        h = self.here
        rows = self.part.shape[2]
        for o in range(1, h.chain):
            self.sent[o].wait_recv()

        def add(i, unused):
            at = pl.ds(pl.multiple_of(i * 16, 16), 16)
            total = self.part[h.a, h.c, at].astype(F32) + self.near[0, at].astype(F32)
            for o in range(1, h.chain):
                total = total + self.far[o, at].astype(F32)
            out[at] = total
            return unused

        lax.fori_loop(0, rows // 16, add, 0)


def fold_offsets(here):
    return chain_offsets(here) + [dict(c=1)]


def push_expand(here, wire, ge_ref, ge_out, first, count):
    made = []
    for a in range(first, first + count):
        for i, (y, b) in enumerate(here.plane()):
            source = ge_ref.at[here.y ^ y, a, here.b ^ b]
            made.append(wire.push(source, ge_out.at[i, a - first], here.to(y=y, b=b)))
    return made


def fourth_kernel(
    part_ref, gr_ref, ge_ref, out_ref, gr_out, ge_out, near, far, send, recv, gsend, grecv
):
    h = Here()
    greet(h, chain_offsets(h) + block_offsets(h))
    wire = Wire(send, recv)
    fold = Fold(h, wire, part_ref, near, far)
    fold.start()
    slot = h.y * h.mid + h.b

    def chunk_copy(b, c):
        device = h.to(b=b, c=c)
        device["dp"] = h.c
        return pltpu.make_async_remote_copy(
            src_ref=gr_ref.at[h.b ^ b, h.c ^ c],
            dst_ref=gr_out.at[slot],
            send_sem=gsend.at[b * h.cores + c],
            recv_sem=grecv.at[slot],
            device_id=device,
            device_id_type=pl.DeviceIdType.MESH,
        )

    far_copies = [chunk_copy(b, c) for b in range(h.mid) for c in range(h.cores) if b or c]
    for copy in far_copies:
        copy.start()

    @pl.when(h.c == h.y)
    def _():
        pltpu.make_async_copy(gr_ref.at[h.b, h.c], gr_out.at[slot], grecv.at[slot]).start()

    @pl.when(h.c != h.y)
    def _():
        chunk_copy(0, 0).start()

    sheets = push_expand(h, wire, ge_ref, ge_out, 0, AHEAD)
    fold.pass_on()
    fold.finish(out_ref)
    for copy in sheets:
        copy.wait_recv()
    for i in range(h.dp * h.mid):
        pltpu.make_async_copy(gr_out.at[i], gr_out.at[i], grecv.at[i]).wait()
    wire.drain()
    for copy in far_copies:
        copy.wait_send()

    @pl.when(h.c != h.y)
    def _():
        chunk_copy(0, 0).wait_send()


AHEAD = 1


def fold_feed(part, gr, ge, sizes):
    dp, chain, mid, cores = sizes
    others = dp * mid - 1
    return call(
        fourth_kernel,
        (
            jax.ShapeDtypeStruct(part.shape[2:], F32),
            jax.ShapeDtypeStruct((dp * mid,) + gr.shape[2:], BF),
            jax.ShapeDtypeStruct((others, AHEAD) + ge.shape[3:], BF),
        ),
        (part, gr, ge),
        Fold.scratch(part)
        + wires(Fold.copies(chain) + others * AHEAD)
        + [pltpu.SemaphoreType.DMA((mid * cores,)), pltpu.SemaphoreType.DMA((dp * mid,))],
        4,
        (VMEM, ANY, ANY),
        [VMEM, ANY, ANY],
    )


class Scatter:
    def __init__(self, here, wire, pick, spots, out, bufs, columns):
        self.here, self.wire, self.pick, self.out = here, wire, pick, out
        self.near, self.sheet, self.line, self.far = bufs
        self.spots, self.columns = spots + [(0, 0)], columns

    @staticmethod
    def copies(spots, chain):
        return (spots + 1) + spots + (chain - 1)

    @staticmethod
    def scratch(spots, chain, rows, width):
        return [
            pltpu.VMEM((spots + 1, chain, rows, width), BF),
            pltpu.VMEM((spots, chain, rows, width), BF),
            pltpu.VMEM((chain, rows, width), BF),
            pltpu.VMEM((chain, rows, width), BF),
        ]

    def start(self):
        h = self.here
        self.swap = [
            self.wire.push(
                self.pick(h.y ^ y, h.b ^ b, h.c ^ 1).at[:, :, self.columns],
                self.near.at[i, :, :, self.columns],
                h.to(c=1),
            )
            for i, (y, b) in enumerate(self.spots)
        ]

    def over_plane(self):
        h = self.here
        self.sent = []
        for i, (y, b) in enumerate(self.spots):
            self.swap[i].wait_recv()
            mine = self.pick(h.y ^ y, h.b ^ b, h.c)

            def add(a, unused):
                total = (
                    mine[a, :, self.columns].astype(F32)
                    + self.near[i, a, :, self.columns].astype(F32)
                )
                self.near[i, a, :, self.columns] = total.astype(BF)
                return unused

            lax.fori_loop(0, h.chain, add, 0)
            if y or b:
                self.sent.append(
                    self.wire.push(
                        self.near.at[i, :, :, self.columns],
                        self.sheet.at[i, :, :, self.columns],
                        h.to(y=y, b=b),
                    )
                )

    def over_chain(self):
        h = self.here
        own = len(self.spots) - 1
        for copy in self.sent:
            copy.wait_recv()
        self.last = []
        for o in list(range(1, h.chain)) + [0]:
            total = self.near[own, h.a ^ o, :, self.columns].astype(F32)
            for i in range(own):
                total = total + self.sheet[i, h.a ^ o, :, self.columns].astype(F32)
            if o:
                self.line[o, :, self.columns] = total.astype(BF)
                self.last.append(
                    self.wire.push(
                        self.line.at[o, :, self.columns],
                        self.far.at[o, :, self.columns],
                        h.to(a=o),
                    )
                )
            else:
                self.out[:, self.columns] = total

    def finish(self):
        h = self.here
        for copy in self.last:
            copy.wait_recv()
        total = self.out[:, self.columns]
        for o in range(1, h.chain):
            total = total + self.far[o, :, self.columns].astype(F32)
        self.out[:, self.columns] = total


def fifth_kernel(
    q_ref, do_ref, lse_ref, delta_ref, kv_ref, part_ref, go_ref, ge_ref,
    dq_ref, dkv_ref, out_ref, go_out, ge_out, made, *rest,
):
    k_bufs, w_bufs, f_bufs, (send, recv, local) = rest[:4], rest[4:8], rest[8:10], rest[10:]
    h = Here()
    span = kv_ref.shape[-2] // KV_HEADS
    load = pltpu.make_async_copy(kv_ref, made, local)
    load.start()
    greet(h, chain_offsets(h) + plane_offsets(h) + [dict(c=1)])
    wire = Wire(send, recv)
    fold = Fold(h, wire, part_ref, *f_bufs)
    fold.start()

    def weight_pick(y, b, c):
        return go_ref.at[y, :, b, c]

    weights = Scatter(
        h, wire, weight_pick, h.plane(), go_out, w_bufs, pl.ds(0, go_ref.shape[-1])
    )
    weights.start()
    fold.pass_on()
    weights.over_plane()
    sheets = push_expand(h, wire, ge_ref, ge_out.at[:, 0:1], AHEAD, 1)

    last = h.rank // 2

    def visit(pair, hide):
        def head(g, unused):
            query, dout = q_ref[g], do_ref[g]
            rows = pl.ds(pl.multiple_of(g * span, span), span)
            spot = (pair // h.mid, lax.rem(pair, h.mid), slice(None), rows)
            keys = made[spot].reshape(2 * span, WIDE)
            probs = jnp.exp(mm(keys, query, NT) - lse_ref[g])
            if hide:
                probs = masked(probs, pair, h.rank, span)
            slope = probs * (mm(keys, dout, NT) - delta_ref[g])
            slope = slope.astype(BF)
            both = mm(slope, query, NN) + mm(probs.astype(BF), dout, NN)
            made[spot] = both.astype(BF).reshape(2, span, WIDE)
            add = mm(keys, slope, TN)[:HD]
            if hide:
                dq_ref[g] = add
            else:
                dq_ref[g] += add
            return unused

        lax.fori_loop(0, KV_HEADS, head, 0)

    load.wait()
    visit(last, True)

    def step(pair, unused):
        visit(pair, False)
        return unused

    lax.fori_loop(0, last, step, 0)

    def clear(pair, unused):
        made[pair // h.mid, lax.rem(pair, h.mid)] = jnp.zeros(made.shape[2:], BF)
        return unused

    lax.fori_loop(last + 1, h.chain * h.mid, clear, 0)

    def key_pick(y, b, c):
        return made.at[:, b, c]

    keys_fold = Scatter(
        h, wire, key_pick, [(0, b) for b in range(1, h.mid)], dkv_ref, k_bufs, pl.ds(0, WIDE)
    )
    keys_fold.start()
    keys_fold.over_plane()
    sheets += push_expand(h, wire, ge_ref, ge_out.at[:, 1:], AHEAD + 1, h.chain - AHEAD - 1)
    weights.over_chain()
    fold.finish(out_ref)
    keys_fold.over_chain()
    weights.finish()
    keys_fold.finish()
    for copy in sheets:
        copy.wait_recv()
    wire.drain()


def attend_backward(query, dout, lse, delta, kv, part, go, ge, sizes):
    dp, chain, mid, cores = sizes
    rows = query.shape[1]
    span = kv.shape[2]
    kv = kv.reshape(chain, mid, cores, KV_HEADS * span, WIDE)
    others = dp * mid - 1
    count = (
        Fold.copies(chain)
        + Scatter.copies(others, chain)
        + Scatter.copies(mid - 1, chain)
        + others * (chain - AHEAD)
    )
    return call(
        fifth_kernel,
        (
            jax.ShapeDtypeStruct((KV_HEADS, HD, rows), F32),
            jax.ShapeDtypeStruct((KV_HEADS * span, WIDE), F32),
            jax.ShapeDtypeStruct(part.shape[2:], F32),
            jax.ShapeDtypeStruct(go.shape[4:], F32),
            jax.ShapeDtypeStruct((others, chain - AHEAD) + ge.shape[3:], BF),
        ),
        (query, dout, lse, delta, kv, part, go, ge),
        [pltpu.VMEM((chain, mid, cores, KV_HEADS * span, WIDE), BF)]
        + Scatter.scratch(mid - 1, chain, KV_HEADS * span, WIDE)
        + Scatter.scratch(others, chain, *go.shape[4:])
        + Fold.scratch(part)
        + wires(count)
        + [pltpu.SemaphoreType.DMA],
        5,
        (VMEM, VMEM, VMEM, VMEM, ANY),
        [VMEM, VMEM, VMEM, VMEM, ANY, VMEM, VMEM, ANY],
    )


def all_offsets(here):
    return [
        dict(y=y, a=a, b=b, c=c)
        for y in range(here.dp)
        for a in range(here.chain)
        for b in range(here.mid)
        for c in range(here.cores)
        if y or a or b or c
    ]


def sixth_kernel(gi_ref, ge_ref, x_ref, gi_out, ge_out, total_ref, *rest):
    bufs, (vector, got, send, recv, local) = rest[:4], rest[4:]
    h = Here()
    greet(h, all_offsets(h))
    wire = Wire(send, recv)
    width = FF // (h.chain * h.cores)
    half_width = gi_ref.shape[-1] // 2

    def pick(y, b, c):
        return gi_ref.at[y, :, b, c]

    jobs = [
        Scatter(h, wire, pick, h.plane(), gi_out, bufs, pl.ds(i * half_width, half_width))
        for i in range(2)
    ]
    for job in jobs:
        job.start()
    kept, swaps = [], []
    chunk = h.c * h.chain + h.a
    for a in range(h.chain):
        for c in range(h.cores):
            for part in range(2):
                source = ge_ref.at[h.a ^ a, h.c ^ c, :, pl.ds(part * width, width)]
                spot = ge_out.at[:, chunk_columns(chunk, part, width)]
                if a or c:
                    swaps.append(wire.push(source, spot, h.to(a=a, c=c)))
                else:
                    copy = pltpu.make_async_copy(source, spot, local.at[part])
                    copy.start()
                    kept.append(copy)
    for job in jobs:
        job.over_plane()
    for job in jobs:
        job.over_chain()
    for job in jobs:
        job.finish()
    squares = jnp.sum(gi_out[...] * gi_out[...])
    last = lax.broadcasted_iota(jnp.int32, x_ref.shape, 0) == x_ref.shape[0] - 1
    vector[...] = x_ref[...] + jnp.where(last, squares, 0.0)
    small = [wire.push(vector, got.at[h.shard], h.to(**offset)) for offset in all_offsets(h)]
    got[h.shard] = vector[...]
    for copy in swaps:
        copy.wait_recv()
    for copy in small:
        copy.wait_recv()
    total_ref[...] = jnp.sum(got[...], axis=0)
    wire.drain()
    for copy in kept:
        copy.wait()


def scatter_projections(gi, ge, x, sizes):
    dp, chain, mid, cores = sizes
    others = dp * mid - 1
    devices = math.prod(sizes)
    count = 2 * Scatter.copies(others, chain) + 2 * (chain * cores - 1) + devices - 1
    return call(
        sixth_kernel,
        (
            jax.ShapeDtypeStruct(gi.shape[4:], F32),
            jax.ShapeDtypeStruct((ge.shape[2], 2 * FF), BF),
            jax.ShapeDtypeStruct(x.shape, F32),
        ),
        (gi, ge, x),
        Scatter.scratch(others, chain, *gi.shape[4:])
        + [pltpu.VMEM(x.shape, F32), pltpu.VMEM((devices,) + x.shape, F32)]
        + wires(count)
        + [pltpu.SemaphoreType.DMA((2,))],
        6,
        (VMEM, ANY, VMEM),
        [VMEM, ANY, VMEM],
    )


def rms_normed(values, gains):
    mean_square = jnp.mean(values * values, axis=-1, keepdims=True)
    return values * lax.rsqrt(mean_square + EPSILON) * gains


def rotary(values, positions):
    half_width = values.shape[-1] // 2
    frequency = THETA ** (-2.0 * jnp.arange(half_width).astype(F32) / values.shape[-1])
    angles = positions.astype(F32)[:, None] * frequency[None, :]
    cosine = jnp.cos(angles)[:, None, :]
    sine_rows = jnp.sin(angles)[:, None, :]
    front_half = values[..., :half_width]
    back_half = values[..., half_width:]
    return jnp.concatenate(
        [front_half * cosine - back_half * sine_rows, back_half * cosine + front_half * sine_rows],
        axis=-1,
    )


def prepare(projected, head_gains, positions):
    row_count = projected.shape[0]
    queries = projected[:, : HEADS * HD].reshape(row_count, HEADS, HD)
    key_rows = projected[:, HEADS * HD : (HEADS + KV_HEADS) * HD].reshape(row_count, KV_HEADS, HD)
    value_rows = projected[:, (HEADS + KV_HEADS) * HD :].reshape(row_count, KV_HEADS, HD)
    queries = rotary(rms_normed(queries, head_gains[0]), positions)
    key_rows = rotary(rms_normed(key_rows, head_gains[1]), positions)
    return (queries, key_rows, value_rows)


def by_group(values):
    rows = values.shape[0]
    values = values.reshape(rows, KV_HEADS, GROUP, HD).transpose(1, 2, 0, 3)
    return values.reshape(KV_HEADS, GROUP * rows, HD)


def by_row(values, rows):
    values = values.reshape(KV_HEADS, HD, GROUP, rows).transpose(3, 0, 2, 1)
    return values.reshape(rows, HEADS * HD)


def on_device(
    sizes,
    tokens,
    cotangent,
    norm_gains,
    head_gains,
    input_weight,
    output_weight,
    expand_weight,
    reduce_weight,
    norm_moment,
    head_moment,
    input_moment,
    output_moment,
    expand_moment,
    reduce_moment,
    learn_rate,
):
    dp, chain, mid, cores = sizes
    seq_count, rows, model_width = tokens.shape
    assert seq_count == 1
    place = (lax.axis_index("a") * mid + lax.axis_index("b")) * cores + lax.axis_index("c")
    positions = place * rows + jnp.arange(rows, dtype=jnp.int32)
    score_scale = 1.0 / math.sqrt(HD)
    upstream_low = cotangent.reshape(rows, model_width)

    full_input, e1 = gather_first(input_weight.astype(BF), expand_weight.astype(BF), sizes)
    full_input = full_input.reshape(model_width, -1)
    input_rows = tokens.reshape(rows, model_width).astype(F32)
    normed_one, norm_one_pull = jax.vjp(rms_normed, input_rows, norm_gains[0])
    normed_one = normed_one.astype(BF)
    projected = jnp.dot(normed_one, full_input, preferred_element_type=F32)

    def prepare_here(projected_rows, gains):
        return prepare(projected_rows, gains, positions)

    (queries, key_rows, value_rows), prepare_pull = jax.vjp(prepare_here, projected, head_gains)
    query_low = by_group((queries.astype(BF) * score_scale).reshape(rows, HEADS * HD))
    query_wide = jnp.pad(query_low, ((0, 0), (0, 0), (0, HD)))
    kv_low = jnp.concatenate([key_rows, value_rows], axis=-1).astype(BF).transpose(1, 0, 2)

    attended_cols, log_mass, kv_all, full_output, cot_all, ex_part = attend_forward(
        query_wide, kv_low, output_weight.astype(BF), upstream_low, e1, sizes
    )
    full_output = full_output.reshape(-1, model_width)
    attended = by_row(attended_cols, rows)
    attended_low = attended.astype(BF)
    branch = jnp.dot(attended_low, full_output, preferred_element_type=F32)
    residual = input_rows + branch
    normed_two, norm_two_pull = jax.vjp(rms_normed, residual, norm_gains[1])
    normed_two = normed_two.astype(BF)

    n_all, rd_all, ex_all = gather_feed(normed_two, e1, reduce_weight.astype(BF), ex_part, sizes)
    n_all = n_all.reshape(-1, model_width)
    cot_all = cot_all.reshape(-1, model_width)
    ex_all = ex_all.reshape(model_width, -1)
    rd_all = rd_all.reshape(-1, model_width)
    part_width = rd_all.shape[0]
    expanded = jnp.dot(n_all, ex_all, preferred_element_type=F32)
    gate_value = expanded[:, :part_width]
    up_value = expanded[:, part_width:]
    sigmoid = jax.nn.sigmoid(gate_value)
    activated = gate_value * sigmoid
    slope = sigmoid * (1.0 + gate_value * (1.0 - sigmoid))
    hidden = (activated * up_value).astype(BF)
    hidden_grad = jnp.einsum("rd,fd->rf", cot_all, rd_all, preferred_element_type=F32)
    expand_grad = jnp.concatenate(
        [hidden_grad * up_value * slope, hidden_grad * activated], axis=1
    ).astype(BF)
    back_part = jnp.einsum("rf,df->rd", expand_grad, ex_all, preferred_element_type=F32).astype(BF)
    grad_reduce = jnp.einsum("rf,rd->fd", hidden, cot_all, preferred_element_type=F32).astype(BF)
    grad_expand = jnp.einsum("rd,rf->df", n_all, expand_grad, preferred_element_type=F32).astype(BF)
    grad_expand = grad_expand.reshape(dp, chain, mid, cores, -1, grad_expand.shape[1])
    normed_two_grad, reduce_got, expand_got = fold_feed(
        back_part.reshape(chain, cores, rows, model_width),
        grad_reduce.reshape(mid, cores, -1, model_width),
        grad_expand,
        sizes,
    )
    out_part = jnp.dot(hidden, rd_all, preferred_element_type=F32).astype(BF)

    def sharded(grad):
        return grad.astype(BF).reshape(dp, chain, mid, cores, -1, grad.shape[1])

    residual_part, gain_two_grad = norm_two_pull(normed_two_grad)
    residual_grad = upstream_low.astype(F32) + residual_part
    branch_grad = residual_grad.astype(BF)
    grad_output = jnp.einsum("rh,rd->hd", attended_low, branch_grad, preferred_element_type=F32)
    attended_grad = jnp.einsum(
        "rd,hd->rh", branch_grad, full_output, preferred_element_type=F32
    ).astype(BF)
    row_delta = jnp.sum(
        (attended_grad.astype(F32) * attended).reshape(rows, KV_HEADS, GROUP, HD), axis=-1
    )
    row_delta = row_delta.transpose(1, 2, 0).reshape(KV_HEADS, 1, GROUP * rows)
    dout_wide = jnp.pad(by_group(attended_grad), ((0, 0), (0, 0), (HD, 0)))
    query_cols, kv_grad, result, shard_output, expand_rest = attend_backward(
        query_wide,
        dout_wide,
        log_mass,
        row_delta,
        kv_all,
        out_part.reshape(chain, cores, rows, model_width),
        sharded(grad_output),
        grad_expand,
        sizes,
    )
    query_grads = by_row(query_cols, rows) * score_scale
    kv_grad = kv_grad.reshape(KV_HEADS, rows, WIDE).transpose(1, 0, 2)
    projected_grad, head_grads = prepare_pull(
        (query_grads.reshape(rows, HEADS, HD), kv_grad[..., :HD], kv_grad[..., HD:])
    )
    projected_low = projected_grad.astype(BF)
    grad_input = jnp.einsum("rd,rc->dc", normed_one, projected_low, preferred_element_type=F32)
    normed_one_grad = jnp.einsum(
        "rc,dc->rd", projected_low, full_input, preferred_element_type=F32
    )
    input_part, gain_one_grad = norm_one_pull(normed_one_grad)
    token_low = (residual_grad + input_part).astype(BF).reshape(tokens.shape)
    layer_out = (residual + result).astype(BF).reshape(tokens.shape)

    y_here, b_here = lax.axis_index("dp"), lax.axis_index("b")
    own_expand = lax.dynamic_index_in_dim(grad_expand, y_here, 0, keepdims=False)
    own_expand = lax.dynamic_index_in_dim(own_expand, b_here, 1, keepdims=False)
    expand_got = jnp.concatenate([expand_got, expand_rest], axis=1)
    sum_expand = own_expand.astype(F32) + jnp.sum(expand_got.astype(F32), axis=0)
    sum_expand = sum_expand.astype(BF)
    sum_wide = sum_expand.astype(F32)
    shard_reduce = jnp.sum(reduce_got.astype(F32), axis=0)
    squares_local = (
        jnp.sum(shard_output * shard_output)
        + jnp.sum(sum_wide * sum_wide)
        + jnp.sum(shard_reduce * shard_reduce)
    )
    gain_count = norm_gains.size
    head_count = head_gains.size
    packed = jnp.concatenate([gain_one_grad, gain_two_grad, head_grads.reshape(-1)])
    packed = packed.reshape(-1, 128)
    packed = jnp.pad(packed, ((0, -(packed.shape[0] + 1) % 8), (0, 0)))
    packed = jnp.concatenate([packed, jnp.full((1, 128), squares_local, F32)])
    shard_input, shard_expand, totals = scatter_projections(
        sharded(grad_input), sum_expand, packed, sizes
    )
    shard_expand = shard_expand.astype(F32)
    square_total = totals[-1, 0]
    totals = totals.reshape(-1)
    gain_totals = totals[:gain_count].reshape(norm_gains.shape)
    head_totals = totals[gain_count : gain_count + head_count].reshape(head_gains.shape)
    grad_norm = jnp.sqrt(
        square_total + jnp.sum(gain_totals * gain_totals) + jnp.sum(head_totals * head_totals)
    )
    clip_limit = math.sqrt(NPARAM)
    factor = clip_limit / jnp.maximum(grad_norm, clip_limit)

    def advance(weight, moment, gradient):
        new_moment = MOMENTUM * moment + factor * gradient
        return (new_moment, weight - learn_rate * new_moment)

    moment_norms, next_norms = advance(norm_gains, norm_moment, gain_totals)
    moment_heads, next_heads = advance(head_gains, head_moment, head_totals)
    moment_input, next_input = advance(input_weight, input_moment, shard_input)
    moment_output, next_output = advance(output_weight, output_moment, shard_output)
    moment_expand, next_expand = advance(expand_weight, expand_moment, shard_expand)
    moment_reduce, next_reduce = advance(reduce_weight, reduce_moment, shard_reduce)
    return (
        layer_out,
        token_low,
        grad_norm,
        moment_norms,
        moment_heads,
        moment_input,
        moment_output,
        moment_expand,
        moment_reduce,
        next_norms,
        next_heads,
        next_input,
        next_output,
        next_expand,
        next_reduce,
    )


def solution(mesh):
    dp, ctx = mesh.shape["dp"], mesh.shape["ctx"]
    sizes = (dp, CHAIN, ctx // (CHAIN * CORES), CORES)
    assert dp == CORES
    grid = Mesh(mesh.devices.reshape(sizes), AXES)
    rows = P("dp", ("a", "b", "c"), None)
    shard = P(AXES, None)
    in_specs = (rows, rows, P(), P(), shard, shard, shard, shard)
    in_specs += (P(), P(), shard, shard, shard, shard, P())
    out_specs = (rows, rows, P(), P(), P(), shard, shard, shard, shard)
    out_specs += (P(), P(), shard, shard, shard, shard)
    return jax.shard_map(
        functools.partial(on_device, sizes),
        mesh=grid,
        in_specs=in_specs,
        out_specs=out_specs,
        check_vma=False,
    )
```
